512 devices in a mesh: dp: 32 (over z, core), expert: 16 (over x, y).
Axes of the slice: x: 4, y: 4, z: 16, core: 2. Of those that a mesh axis runs over, the one named last changes fastest.
Arguments:
- tokens: bfloat16 [5120, 4096], P('expert', 'dp'), may hold values from -6 to 6
- out_grad: bfloat16 [5120, 4096], P('expert', 'dp'), may hold values from -0.29882812 to 0.29882812
- slot_tokens: int32 [4, 160], replicated, may hold values from 0 to 5119, as said below
- slot_gate: float32 [4, 160], replicated, may hold values from 0.1 to 1
- w_gate: bfloat16 [16, 4096, 2048], P('expert', 'dp'), may hold values from -0.09375 to 0.09375
- w_up: bfloat16 [16, 4096, 2048], P('expert', 'dp'), may hold values from -0.09375 to 0.09375
- w_down: bfloat16 [16, 2048, 4096], P('expert', None, 'dp'), may hold values from -0.0625 to 0.0625
Outputs:
- grad_tokens: bfloat16 [5120, 4096], P('expert', 'dp')
- grad_w_gate: bfloat16 [16, 4096, 2048], P('expert', 'dp')
- grad_w_up: bfloat16 [16, 4096, 2048], P('expert', 'dp')
- grad_w_down: bfloat16 [16, 2048, 4096], P('expert', None, 'dp')
- grad_gates: float32 [16, 40], P('expert')
The draws below stay inside these ranges and needn't reach their ends.
Inputs may be any that keep to these rules, and one draw needn't show every extreme that they name: `slot_tokens`: row e lists 160 distinct token numbers, ordered by their owner t // 320 ascending. At most 20 of a row come from the 320 tokens of one owner, and in every row exactly 20 come from one owner.
All inputs are finite; a program needn't handle non-finite values.
Results may differ from the reference program's by a relative error of at most 0.0057.
Values may be sent and summed in bfloat16 or wider, within the bound.
No kernel may reach another device: no remote copies, remote signals or barrier semaphores. Data moves between devices by JAX's collectives and lax.ppermute only.
A program may use at most 64 MiB of HBM per device.

```python
from functools import partial
import jax
import jax.numpy as jnp
from jax import lax

D = 4096
FF_WIN = 8192
GROUP = 4
TOK_DEV = 320
TOKENS = 5120
FLIGHT = 4
FF_Q = 2048
CAP = 160
MOST = 20
N_EXPERT = 16


def draw_slot_tokens(key, part):
    key_hot = jax.random.fold_in(key, 11)
    key_pick = jax.random.fold_in(key, 12)
    key_order = jax.random.fold_in(key, 13)
    hot_owner = jax.random.randint(key_hot, (FLIGHT,), 0, N_EXPERT, dtype=jnp.int32)
    spare_slots = MOST - 1
    candidates = (N_EXPERT - 1) * spare_slots
    pick_keys = jax.random.split(key_pick, FLIGHT)
    orders = jax.vmap(partial(jax.random.permutation, x=candidates))(pick_keys)
    chosen = orders[:, :CAP - MOST].astype(jnp.int32)
    offset = chosen // spare_slots
    owner_of = (hot_owner[:, None] + 1 + offset) % N_EXPERT
    owner_range = jnp.arange(N_EXPERT, dtype=jnp.int32)
    counts = jnp.sum((owner_of[:, :, None] == owner_range[None, None, :]).astype(jnp.int32), axis=1)
    counts = counts + MOST * (owner_range[None, :] == hot_owner[:, None]).astype(jnp.int32)
    bucket_ends = jnp.cumsum(counts, axis=1)
    bucket_starts = bucket_ends - counts
    slot_range = jnp.arange(CAP, dtype=jnp.int32)
    owner_slot = jnp.sum((bucket_ends[:, None, :] <= slot_range[None, :, None]).astype(jnp.int32), axis=2)
    start_slot = jnp.take_along_axis(bucket_starts, owner_slot, axis=1)
    rank_slot = slot_range[None, :] - start_slot
    order_keys = jax.random.split(key_order, FLIGHT * N_EXPERT)
    local_orders = jax.vmap(partial(jax.random.permutation, x=TOK_DEV))(order_keys)
    local_orders = local_orders.reshape(FLIGHT, N_EXPERT, TOK_DEV).astype(jnp.int32)
    expert_range = jnp.arange(FLIGHT, dtype=jnp.int32)[:, None]
    local_token = local_orders[expert_range, owner_slot, rank_slot]
    return (owner_slot * TOK_DEV + local_token).astype(jnp.int32)


def block_scale(key, extent, pieces, least, top_value):
    factor_of, own = 1.0, jax.random.fold_in(key, 6)
    for dim, shards_of in pieces:
        heights = jnp.exp(jax.random.uniform(jax.random.fold_in(own, dim), (shards_of,), jnp.float32, least / len(pieces), top_value / len(pieces)))
        factor_of = factor_of * jnp.repeat(heights, extent[dim] // shards_of).reshape([-1 if axis == dim else 1 for axis in range(len(extent))])
    return factor_of


def gaussian(own_key, dims, width, bound, shards=(), kind=jnp.bfloat16):
    gain = block_scale(own_key, dims, shards, -0.22, 0.18) if shards else 1.0
    result = jax.random.normal(own_key, dims, jnp.float32) * width * gain
    return jnp.minimum(jnp.maximum(result, -bound), bound).astype(kind)


def setup_inputs(seed: int = 0) -> dict:
    arg_keys = jax.random.split(jax.random.key(seed), 8)
    tokens = gaussian(arg_keys[0], (TOKENS, D), 1.0, 6.0, ((0, 16), (1, 32)))
    out_grad = gaussian(arg_keys[1], (TOKENS, D), 0.05, 0.29882812, ((0, 16), (1, 32)))
    slot_tokens = draw_slot_tokens(jax.random.fold_in(arg_keys[7], 71), 0)
    slot_gate = jnp.clip(jax.random.uniform(arg_keys[3], (FLIGHT, CAP), jnp.float32, 0.1, 1.0), 0.1, 1.0)
    w_gate = gaussian(arg_keys[4], (FLIGHT * GROUP, D, FF_Q), D ** -0.5, 0.09375, ((0, 16), (1, 32)))
    w_up = gaussian(arg_keys[5], (FLIGHT * GROUP, D, FF_Q), D ** -0.5, 0.09375, ((0, 16), (1, 32)))
    w_down = gaussian(arg_keys[6], (FLIGHT * GROUP, FF_Q, D), FF_WIN ** -0.5, 0.0625, ((0, 16), (2, 32)))
    return dict(tokens=tokens, out_grad=out_grad, slot_tokens=slot_tokens, slot_gate=slot_gate, w_gate=w_gate, w_up=w_up, w_down=w_down)


def reference(tokens, out_grad, slot_tokens, slot_gate, w_gate, w_up, w_down):
    gate_parts_all = w_gate.reshape(FLIGHT, GROUP, D, FF_Q)
    up_parts_all = w_up.reshape(FLIGHT, GROUP, D, FF_Q)
    down_parts_all = w_down.reshape(FLIGHT, GROUP * FF_Q, D)

    def one_expert(operands):
        chosen, gates, gate_parts, up_parts, down_matrix = operands
        gate_matrix = jnp.transpose(gate_parts, (1, 0, 2)).reshape(D, FF_WIN)
        up_matrix = jnp.transpose(up_parts, (1, 0, 2)).reshape(D, FF_WIN)
        slot_inputs = tokens[chosen]
        slot_grads = out_grad[chosen]
        pre_gate = jnp.dot(slot_inputs, gate_matrix, preferred_element_type=jnp.float32)
        pre_up = jnp.dot(slot_inputs, up_matrix, preferred_element_type=jnp.float32)
        sigmoid_gate = jax.nn.sigmoid(pre_gate)
        hidden = (pre_gate * sigmoid_gate * pre_up).astype(jnp.bfloat16)
        expert_out = jnp.dot(hidden, down_matrix, preferred_element_type=jnp.float32)
        gate_grad = jnp.sum(slot_grads.astype(jnp.float32) * expert_out, axis=1)
        scaled = (gates[:, None] * slot_grads.astype(jnp.float32)).astype(jnp.bfloat16)
        down_grad = jnp.dot(hidden.T, scaled, preferred_element_type=jnp.float32).astype(jnp.bfloat16)
        hidden_grad = jnp.dot(scaled, down_matrix.T, preferred_element_type=jnp.float32)
        gate_side = (hidden_grad * pre_up * sigmoid_gate * (1.0 + pre_gate * (1.0 - sigmoid_gate))).astype(jnp.bfloat16)
        up_side = (hidden_grad * pre_gate * sigmoid_gate).astype(jnp.bfloat16)
        gate_w_grad = jnp.dot(slot_inputs.T, gate_side, preferred_element_type=jnp.float32).astype(jnp.bfloat16)
        up_w_grad = jnp.dot(slot_inputs.T, up_side, preferred_element_type=jnp.float32).astype(jnp.bfloat16)
        input_grad = jnp.dot(gate_side, gate_matrix.T, preferred_element_type=jnp.float32)
        input_grad = input_grad + jnp.dot(up_side, up_matrix.T, preferred_element_type=jnp.float32)
        gate_w_grad = jnp.transpose(gate_w_grad.reshape(D, GROUP, FF_Q), (1, 0, 2))
        up_w_grad = jnp.transpose(up_w_grad.reshape(D, GROUP, FF_Q), (1, 0, 2))
        return gate_w_grad, up_w_grad, down_grad.reshape(GROUP, FF_Q, D), input_grad, gate_grad

    results = lax.map(one_expert, (slot_tokens, slot_gate, gate_parts_all, up_parts_all, down_parts_all))
    gate_w_grads, up_w_grads, down_grads, input_grads, gate_grads = results
    summed = jnp.zeros((TOKENS, D), jnp.float32).at[slot_tokens.reshape(-1)].add(input_grads.reshape(FLIGHT * CAP, D))
    grad_tokens = summed.astype(jnp.bfloat16)
    grad_w_gate = gate_w_grads.reshape(FLIGHT * GROUP, D, FF_Q)
    grad_w_up = up_w_grads.reshape(FLIGHT * GROUP, D, FF_Q)
    grad_w_down = down_grads.reshape(FLIGHT * GROUP, FF_Q, D)
    grad_gates = gate_grads.reshape(FLIGHT * GROUP, CAP // GROUP)
    return (grad_tokens, grad_w_gate, grad_w_up, grad_w_down, grad_gates)
```

```python
import jax
import jax.numpy as jnp
import numpy as np
from jax import lax
from jax.experimental import pallas as pl
from jax.experimental.pallas import tpu as pltpu
from jax.sharding import Mesh
from jax.sharding import PartitionSpec as P

BF16 = jnp.bfloat16
F32 = jnp.float32
I32 = jnp.int32

TOK = 320
CAP = 160
HALF = 80
OWNERS = 16
FLIGHT = 4
ROOM = 24
LANES = 128
BLOCKS = 16
PIECE = 3 * HALF + 8

VMEM = pl.BlockSpec(memory_space=pltpu.VMEM)


def iota(shape, dim):
    return lax.broadcasted_iota(I32, shape, dim)


def dot(left, right, left_dim=1, right_dim=0, precision=None):
    return lax.dot_general(
        left,
        right,
        (((left_dim,), (right_dim,)), ((), ())),
        preferred_element_type=F32,
        precision=precision,
    )


def owned_tokens(row, first, rows):
    start = jnp.sum((row < first).astype(I32), axis=1, keepdims=True)
    count = jnp.sum(((row >= first) & (row < first + TOK)).astype(I32), axis=1, keepdims=True)
    rank = lax.rem(iota((rows, CAP), 0), ROOM)
    chosen = (iota((rows, CAP), 1) == start + rank) & (rank < count)
    token = jnp.sum(jnp.where(chosen, row - first + 1, 0), axis=1, keepdims=True)
    return token - 1


def column(row, core):
    slot = lax.rem(iota((CAP, CAP), 0) + HALF * core, CAP)
    return jnp.sum(jnp.where(iota((CAP, CAP), 1) == slot, row, 0), axis=1, keepdims=True)


def places(row, core):
    token = column(row, core)
    owner = jnp.sum(
        ((iota((CAP, LANES), 1) < OWNERS - 1) & (token >= TOK * (iota((CAP, LANES), 1) + 1))).astype(I32),
        axis=1,
        keepdims=True,
    )
    start = jnp.sum((row < TOK * owner).astype(I32), axis=1, keepdims=True)
    slot = lax.rem(iota((CAP, 1), 0) + HALF * core, CAP)
    return owner, slot - start


def dispatch_kernel(slots_ref, tokens_ref, grads_ref, send_ref):
    first = TOK * (4 * lax.axis_index("x") + lax.axis_index("y"))
    rows = 2 * ROOM
    for expert in range(FLIGHT):
        local = owned_tokens(slots_ref[expert : expert + 1, :], first, rows)
        hit = local == iota((rows, TOK), 1)
        upper = iota((rows, TOK), 0) < ROOM
        pick_tokens = jnp.where(hit & upper, 1.0, 0.0).astype(BF16)
        pick_grads = jnp.where(hit & ~upper, 1.0, 0.0).astype(BF16)
        rows_out = (dot(pick_tokens, tokens_ref[...]) + dot(pick_grads, grads_ref[...])).astype(BF16)
        for part in range(4):
            send_ref[4 * expert + part] = rows_out


def front_kernel(
    slots_ref, gates_ref, recv_ref, gate_ref, up_ref, down_ref, keep_ref, send_ref, inputs_ref, scaled_ref
):
    expert = lax.axis_index("x")
    core = lax.axis_index("core")
    row = slots_ref[pl.ds(expert, 1), :]
    owner, rank = places(row, core)
    place = owner * (2 * ROOM) + rank
    width = OWNERS * 2 * ROOM
    recv = recv_ref[...].reshape(width, LANES)
    where = iota((CAP, width), 1)
    inputs = dot(jnp.where(where == place, 1.0, 0.0).astype(BF16), recv).astype(BF16)
    grads = dot(jnp.where(where == place + ROOM, 1.0, 0.0).astype(BF16), recv)
    gates = column(gates_ref[pl.ds(expert, 1), :], core)
    scaled = (gates * grads).astype(BF16)
    inputs_ref[...] = inputs
    scaled_ref[...] = scaled
    for pair in range(BLOCKS // 2):
        cols = slice(256 * pair, 256 * pair + 256)
        sums = (
            dot(inputs, gate_ref[:, cols]),
            dot(inputs, up_ref[:, cols]),
            dot(scaled, down_ref[cols, :], 1, 1),
        )
        for which, total in enumerate(sums):
            for side in range(2):
                lanes = slice(LANES * side, LANES * side + LANES)
                rows = slice(HALF * which, HALF * which + HALF)
                keep_ref[2 * pair + side, rows, :] = total[:HALF, lanes]
                send_ref[2 * pair + side, rows, :] = total[HALF:, lanes]


def middle_kernel(gates_ref, parts_ref, out_ref):
    core = lax.axis_index("core")
    gates = column(gates_ref[pl.ds(lax.axis_index("x"), 1), :], core)[:HALF]

    def total(which):
        rows = slice(HALF * which, HALF * which + HALF)
        result = parts_ref[0, rows, :].astype(F32)
        for block in range(1, BLOCKS):
            result = result + parts_ref[block, rows, :].astype(F32)
        return result

    pre_gate, pre_up, upstream = total(0), total(1), total(2)
    sigmoid = jax.nn.sigmoid(pre_gate)
    hidden = (pre_gate * sigmoid * pre_up).astype(BF16)
    out_ref[:HALF, :] = hidden
    out_ref[HALF : 2 * HALF, :] = (upstream * pre_up * sigmoid * (1.0 + pre_gate * (1.0 - sigmoid))).astype(BF16)
    out_ref[2 * HALF : 3 * HALF, :] = (upstream * pre_gate * sigmoid).astype(BF16)
    part = jnp.sum(hidden.astype(F32) * upstream, axis=1, keepdims=True) / gates
    eye = iota((HALF, LANES), 0) == iota((HALF, LANES), 1)
    part = jnp.sum(jnp.where(eye, part, 0.0), axis=0, keepdims=True)
    high = part.astype(BF16).astype(F32)
    line = iota((8, LANES), 0)
    tail = jnp.where(line == 0, high, jnp.where(line == 1, part - high, 0.0))
    out_ref[3 * HALF :, :] = tail.astype(BF16)


def back_kernel(
    slots_ref,
    inputs_ref,
    scaled_ref,
    mine_ref,
    other_ref,
    gate_ref,
    up_ref,
    grad_gate_ref,
    grad_up_ref,
    grad_down_ref,
    send_ref,
):
    core = lax.axis_index("core")
    inputs = inputs_ref[...]
    scaled = scaled_ref[...]

    def joined(which, pair):
        rows = slice(HALF * which, HALF * which + HALF)
        sides = [
            jnp.concatenate([mine_ref[block, rows, :], other_ref[block, rows, :]], axis=0)
            for block in (2 * pair, 2 * pair + 1)
        ]
        return jnp.concatenate(sides, axis=1)

    back = jnp.zeros((CAP, LANES), F32)
    for pair in range(BLOCKS // 2):
        cols = slice(256 * pair, 256 * pair + 256)
        hidden, gate_side, up_side = joined(0, pair), joined(1, pair), joined(2, pair)
        grad_gate_ref[:, cols] = dot(inputs, gate_side, 0, 0).astype(BF16)
        grad_up_ref[:, cols] = dot(inputs, up_side, 0, 0).astype(BF16)
        grad_down_ref[cols, :] = dot(hidden, scaled, 0, 0).astype(BF16)
        back = back + dot(gate_side, gate_ref[:, cols], 1, 1) + dot(up_side, up_ref[:, cols], 1, 1)

    row = slots_ref[pl.ds(lax.axis_index("x"), 1), :]
    owner, rank = places(row, core)
    spread = jnp.where(iota((CAP, OWNERS * ROOM), 1) == owner * ROOM + rank, 1.0, 0.0)
    buckets = dot(spread, back, 0, 0, lax.Precision.HIGHEST).reshape(OWNERS, ROOM, LANES)

    def gate_row(ref):
        lines = jnp.zeros((8, LANES), F32)
        for block in range(BLOCKS):
            lines = lines + ref[block, 3 * HALF :, :].astype(F32)
        return jnp.broadcast_to(jnp.sum(lines, axis=0, keepdims=True), (8, LANES))

    gates_mine, gates_other = gate_row(mine_ref), gate_row(other_ref)
    line = iota((8, LANES), 0)
    for quarter in range(4):
        slot = iota((LANES, LANES), 1) + 40 * quarter
        place = lax.rem(slot + HALF * core, CAP)
        source = iota((LANES, LANES), 0)
        valid = iota((LANES, LANES), 1) < 40
        take_mine = jnp.where(valid & (place < HALF) & (source == place), 1.0, 0.0)
        take_other = jnp.where(valid & (place >= HALF) & (source == place - HALF), 1.0, 0.0)
        gates = dot(gates_mine, take_mine, precision=lax.Precision.HIGHEST) + dot(
            gates_other, take_other, precision=lax.Precision.HIGHEST
        )
        for expert in range(FLIGHT):
            bucket = buckets[4 * expert + quarter]
            send_ref[4 * expert + quarter, :16, :] = bucket[:16]
            send_ref[4 * expert + quarter, 16:, :] = jnp.where(line == 4, gates, bucket[16:])


def last_kernel(slots_ref, incoming_ref, tokens_ref, gates_ref):
    expert_here = lax.axis_index("x")
    first = TOK * (4 * expert_here + lax.axis_index("y"))
    total = jnp.zeros((TOK, LANES), F32)
    for expert in range(FLIGHT):
        local = owned_tokens(slots_ref[expert : expert + 1, :], first, ROOM)
        pick = jnp.where(local == iota((ROOM, TOK), 1), 1.0, 0.0)
        rows = incoming_ref[4 * expert]
        for part in range(1, 4):
            rows = rows + incoming_ref[4 * expert + part]
        total = total + dot(pick, rows, 0, 0, lax.Precision.HIGHEST)
    tokens_ref[...] = total.astype(BF16)
    gates = incoming_ref[4 * expert_here, 16:, :]
    for part in range(1, 4):
        gates = gates + incoming_ref[4 * expert_here + part, 16:, :]
    gates_ref[...] = gates[4:5, :]


def call(kernel, out_shape, inputs):
    return pl.pallas_call(
        kernel,
        out_shape=out_shape,
        in_specs=[VMEM] * len(inputs),
        out_specs=jax.tree.map(lambda _: VMEM, out_shape),
    )(*inputs)


def shape(dims, kind):
    return jax.ShapeDtypeStruct(dims, kind)


def swap_cores(value):
    return lax.ppermute(value, "core", [(0, 1), (1, 0)])


def per_device(tokens, out_grad, slot_tokens, slot_gate, w_gate, w_up, w_down):
    gate_weight, up_weight, down_weight = w_gate[0], w_up[0], w_down[0]
    send = call(
        dispatch_kernel,
        shape((OWNERS, 2 * ROOM, LANES), BF16),
        (slot_tokens, tokens, out_grad),
    )
    recv = lax.all_to_all(send, ("x", "y"), split_axis=0, concat_axis=0, tiled=True)
    halves = shape((BLOCKS, 3 * HALF, LANES), F32)
    rows = shape((CAP, LANES), BF16)
    keep, give, inputs, scaled = call(
        front_kernel,
        (halves, halves, rows, rows),
        (slot_tokens, slot_gate, recv, gate_weight, up_weight, down_weight),
    )
    sums = (keep + swap_cores(give)).astype(BF16)
    parts = lax.all_to_all(sums, "z", split_axis=0, concat_axis=0, tiled=True)
    piece = call(middle_kernel, shape((PIECE, LANES), BF16), (slot_gate, parts))
    mine = lax.all_gather(piece, "z", axis=0, tiled=False)
    other = swap_cores(mine)
    grad_gate, grad_up, grad_down, outgoing = call(
        back_kernel,
        (
            shape(gate_weight.shape, BF16),
            shape(up_weight.shape, BF16),
            shape(down_weight.shape, BF16),
            shape((OWNERS, ROOM, LANES), F32),
        ),
        (slot_tokens, inputs, scaled, mine, other, gate_weight, up_weight),
    )
    incoming = lax.all_to_all(outgoing, ("x", "y"), split_axis=0, concat_axis=0, tiled=True)
    grad_tokens, gate_line = call(
        last_kernel,
        (shape((TOK, LANES), BF16), shape((1, LANES), F32)),
        (slot_tokens, incoming),
    )
    return (grad_tokens, grad_gate[None], grad_up[None], grad_down[None], gate_line[:, :40])


def solution(mesh):
    torus = Mesh(mesh.devices.reshape(16, 2, 4, 4), ("z", "core", "x", "y"))
    dp, expert = ("z", "core"), ("x", "y")
    in_specs = (
        P(expert, dp),
        P(expert, dp),
        P(),
        P(),
        P(expert, dp, None),
        P(expert, dp, None),
        P(expert, None, dp),
    )
    out_specs = (
        P(expert, dp),
        P(expert, dp, None),
        P(expert, dp, None),
        P(expert, None, dp),
        P(expert, None),
    )
    return jax.shard_map(
        per_device, mesh=torus, in_specs=in_specs, out_specs=out_specs, check_vma=False
    )
```

```python
import jax
import jax.numpy as jnp
from jax import lax
from jax.experimental import pallas as pl
from jax.experimental.pallas import tpu as pltpu
from jax.sharding import Mesh
from jax.sharding import PartitionSpec as P

BF16 = jnp.bfloat16
F32 = jnp.float32
I32 = jnp.int32

TOK = 320
CAP = 160
HALF = 80
OWNERS = 16
FLIGHT = 4
MOST = 20
ROOM = 24
LANES = 128
BLOCKS = 16
PIECE = 3 * HALF + 8

VMEM = pl.BlockSpec(memory_space=pltpu.VMEM)


def iota(shape, dim):
    return lax.broadcasted_iota(I32, shape, dim)


def dot(left, right, left_dim=1, right_dim=0, precision=None):
    return lax.dot_general(
        left,
        right,
        (((left_dim,), (right_dim,)), ((), ())),
        preferred_element_type=F32,
        precision=precision,
    )


def owned_tokens(row, first, rows, room):
    start = jnp.sum((row < first).astype(I32), axis=1, keepdims=True)
    count = jnp.sum(((row >= first) & (row < first + TOK)).astype(I32), axis=1, keepdims=True)
    rank = lax.rem(iota((rows, CAP), 0), room)
    chosen = (iota((rows, CAP), 1) == start + rank) & (rank < count)
    token = jnp.sum(jnp.where(chosen, row - first + 1, 0), axis=1, keepdims=True)
    return token - 1


def column(row, core):
    slot = lax.rem(iota((CAP, CAP), 0) + HALF * core, CAP)
    return jnp.sum(jnp.where(iota((CAP, CAP), 1) == slot, row, 0), axis=1, keepdims=True)


def places(row, core):
    token = column(row, core)
    owner = jnp.sum(
        ((iota((CAP, LANES), 1) < OWNERS - 1) & (token >= TOK * (iota((CAP, LANES), 1) + 1))).astype(I32),
        axis=1,
        keepdims=True,
    )
    start = jnp.sum((row < TOK * owner).astype(I32), axis=1, keepdims=True)
    slot = lax.rem(iota((CAP, 1), 0) + HALF * core, CAP)
    return owner, slot - start


def dispatch_kernel(slots_ref, tokens_ref, grads_ref, send_ref):
    first = TOK * (4 * lax.axis_index("x") + lax.axis_index("y"))
    rows = 2 * MOST
    for expert in range(FLIGHT):
        local = owned_tokens(slots_ref[expert : expert + 1, :], first, rows, MOST)
        hit = local == iota((rows, TOK), 1)
        upper = iota((rows, TOK), 0) < MOST
        pick_tokens = jnp.where(hit & upper, 1.0, 0.0).astype(BF16)
        pick_grads = jnp.where(hit & ~upper, 1.0, 0.0).astype(BF16)
        rows_out = (dot(pick_tokens, tokens_ref[...]) + dot(pick_grads, grads_ref[...])).astype(BF16)
        for part in range(4):
            send_ref[4 * expert + part] = rows_out


def front_kernel(
    slots_ref, gates_ref, recv_ref, gate_ref, up_ref, down_ref, keep_ref, send_ref, inputs_ref, scaled_ref
):
    expert = lax.axis_index("x")
    core = lax.axis_index("core")
    row = slots_ref[pl.ds(expert, 1), :]
    owner, rank = places(row, core)
    place = owner * (2 * MOST) + rank
    width = OWNERS * 2 * MOST
    recv = recv_ref[...].reshape(width, LANES)
    where = iota((CAP, width), 1)
    inputs = dot(jnp.where(where == place, 1.0, 0.0).astype(BF16), recv).astype(BF16)
    grads = dot(jnp.where(where == place + MOST, 1.0, 0.0).astype(BF16), recv)
    gates = column(gates_ref[pl.ds(expert, 1), :], core)
    scaled = (gates * grads).astype(BF16)
    inputs_ref[...] = inputs
    scaled_ref[...] = scaled
    for pair in range(BLOCKS // 2):
        cols = slice(256 * pair, 256 * pair + 256)
        sums = (
            dot(inputs, gate_ref[:, cols]),
            dot(inputs, up_ref[:, cols]),
            dot(scaled, down_ref[cols, :], 1, 1),
        )
        for which, total in enumerate(sums):
            for side in range(2):
                lanes = slice(LANES * side, LANES * side + LANES)
                rows = slice(HALF * which, HALF * which + HALF)
                keep_ref[2 * pair + side, rows, :] = total[:HALF, lanes]
                send_ref[2 * pair + side, rows, :] = total[HALF:, lanes]


def pair_kernel(keep_ref, recv_ref, sums_ref, own_ref):
    for block in range(BLOCKS):
        sums_ref[block] = (keep_ref[block] + recv_ref[block]).astype(BF16)
    first = 4 * lax.axis_index("zl")
    for block in range(4):
        own_ref[block] = keep_ref[first + block] + recv_ref[first + block]


def others(parts_ref, axis, own, index):
    here = lax.axis_index(axis)
    for step in range(1, 4):
        own = own + parts_ref[(lax.rem(here + step, 4), *index)].astype(F32)
    return own


def near_kernel(parts_ref, own_ref, sums_ref, left_ref):
    for block in range(4):
        sums_ref[block] = others(parts_ref, "zl", own_ref[block], (block,)).astype(BF16)
    block = lax.axis_index("zh")
    left_ref[...] = others(parts_ref, "zl", own_ref[block], (block,))


def middle_kernel(gates_ref, parts_ref, own_ref, out_ref):
    core = lax.axis_index("core")
    gates = column(gates_ref[pl.ds(lax.axis_index("x"), 1), :], core)[:HALF]

    def total(which):
        rows = slice(HALF * which, HALF * which + HALF)
        return others(parts_ref, "zh", own_ref[rows, :], (rows,))

    pre_gate, pre_up, upstream = total(0), total(1), total(2)
    sigmoid = jax.nn.sigmoid(pre_gate)
    hidden = (pre_gate * sigmoid * pre_up).astype(BF16)
    out_ref[:HALF, :] = hidden
    out_ref[HALF : 2 * HALF, :] = (upstream * pre_up * sigmoid * (1.0 + pre_gate * (1.0 - sigmoid))).astype(BF16)
    out_ref[2 * HALF : 3 * HALF, :] = (upstream * pre_gate * sigmoid).astype(BF16)
    part = jnp.sum(hidden.astype(F32) * upstream, axis=1, keepdims=True) / gates
    eye = iota((HALF, LANES), 0) == iota((HALF, LANES), 1)
    part = jnp.sum(jnp.where(eye, part, 0.0), axis=0, keepdims=True)
    high = part.astype(BF16).astype(F32)
    line = iota((8, LANES), 0)
    tail = jnp.where(line == 0, high, jnp.where(line == 1, part - high, 0.0))
    out_ref[3 * HALF :, :] = tail.astype(BF16)


def holder(block):
    return 4 * (block % 4) + block // 4


def back_kernel(
    slots_ref,
    inputs_ref,
    scaled_ref,
    mine_ref,
    other_ref,
    gate_ref,
    up_ref,
    grad_gate_ref,
    grad_up_ref,
    grad_down_ref,
    send_ref,
):
    core = lax.axis_index("core")
    inputs = inputs_ref[...]
    scaled = scaled_ref[...]

    def joined(which, pair):
        rows = slice(HALF * which, HALF * which + HALF)
        sides = [
            jnp.concatenate([mine_ref[place, rows, :], other_ref[place, rows, :]], axis=0)
            for place in (holder(2 * pair), holder(2 * pair + 1))
        ]
        return jnp.concatenate(sides, axis=1)

    back = jnp.zeros((CAP, LANES), F32)
    for pair in range(BLOCKS // 2):
        cols = slice(256 * pair, 256 * pair + 256)
        hidden, gate_side, up_side = joined(0, pair), joined(1, pair), joined(2, pair)
        grad_gate_ref[:, cols] = dot(inputs, gate_side, 0, 0).astype(BF16)
        grad_up_ref[:, cols] = dot(inputs, up_side, 0, 0).astype(BF16)
        grad_down_ref[cols, :] = dot(hidden, scaled, 0, 0).astype(BF16)
        back = back + dot(gate_side, gate_ref[:, cols], 1, 1) + dot(up_side, up_ref[:, cols], 1, 1)

    row = slots_ref[pl.ds(lax.axis_index("x"), 1), :]
    owner, rank = places(row, core)
    spread = jnp.where(iota((CAP, OWNERS * ROOM), 1) == owner * ROOM + rank, 1.0, 0.0)
    buckets = dot(spread, back, 0, 0, lax.Precision.HIGHEST).reshape(OWNERS, ROOM, LANES)

    def gate_row(ref):
        lines = jnp.zeros((8, LANES), F32)
        for block in range(BLOCKS):
            lines = lines + ref[block, 3 * HALF :, :].astype(F32)
        return jnp.broadcast_to(jnp.sum(lines, axis=0, keepdims=True), (8, LANES))

    gates_mine, gates_other = gate_row(mine_ref), gate_row(other_ref)
    line = iota((8, LANES), 0)
    for quarter in range(4):
        slot = iota((LANES, LANES), 1) + 40 * quarter
        place = lax.rem(slot + HALF * core, CAP)
        source = iota((LANES, LANES), 0)
        valid = iota((LANES, LANES), 1) < 40
        take_mine = jnp.where(valid & (place < HALF) & (source == place), 1.0, 0.0)
        take_other = jnp.where(valid & (place >= HALF) & (source == place - HALF), 1.0, 0.0)
        gates = dot(gates_mine, take_mine, precision=lax.Precision.HIGHEST) + dot(
            gates_other, take_other, precision=lax.Precision.HIGHEST
        )
        for expert in range(FLIGHT):
            bucket = buckets[4 * expert + quarter]
            send_ref[4 * expert + quarter, :16, :] = bucket[:16]
            send_ref[4 * expert + quarter, 16:, :] = jnp.where(line == 4, gates, bucket[16:])


def last_kernel(slots_ref, incoming_ref, tokens_ref, gates_ref):
    expert_here = lax.axis_index("x")
    first = TOK * (4 * expert_here + lax.axis_index("y"))
    total = jnp.zeros((TOK, LANES), F32)
    for expert in range(FLIGHT):
        local = owned_tokens(slots_ref[expert : expert + 1, :], first, ROOM, ROOM)
        pick = jnp.where(local == iota((ROOM, TOK), 1), 1.0, 0.0)
        rows = incoming_ref[4 * expert]
        for part in range(1, 4):
            rows = rows + incoming_ref[4 * expert + part]
        total = total + dot(pick, rows, 0, 0, lax.Precision.HIGHEST)
    tokens_ref[...] = total.astype(BF16)
    gates = incoming_ref[4 * expert_here, 16:, :]
    for part in range(1, 4):
        gates = gates + incoming_ref[4 * expert_here + part, 16:, :]
    gates_ref[...] = gates[4:5, :]


def call(kernel, out_shape, inputs):
    return pl.pallas_call(
        kernel,
        out_shape=out_shape,
        in_specs=[VMEM] * len(inputs),
        out_specs=jax.tree.map(lambda _: VMEM, out_shape),
        compiler_params=pltpu.CompilerParams(vmem_limit_bytes=24 << 20),
    )(*inputs)


def shape(dims, kind):
    return jax.ShapeDtypeStruct(dims, kind)


def on_chip(dims, kind):
    return pltpu.VMEM(dims, kind)


def near(value):
    return pltpu.with_memory_space_constraint(value, pltpu.VMEM)


def swap_cores(value):
    return lax.ppermute(value, "core", [(0, 1), (1, 0)])


def per_device(tokens, out_grad, slot_tokens, slot_gate, w_gate, w_up, w_down):
    gate_weight, up_weight, down_weight = w_gate[0], w_up[0], w_down[0]
    send = call(
        dispatch_kernel,
        on_chip((OWNERS, 2 * MOST, LANES), BF16),
        (slot_tokens, tokens, out_grad),
    )
    recv = lax.all_to_all(send, ("x", "y"), split_axis=0, concat_axis=0, tiled=True)
    halves = on_chip((BLOCKS, 3 * HALF, LANES), F32)
    rows = on_chip((CAP, LANES), BF16)
    keep, give, inputs, scaled = call(
        front_kernel,
        (halves, halves, rows, rows),
        (slot_tokens, slot_gate, near(recv), gate_weight, up_weight, down_weight),
    )
    sums, own = call(
        pair_kernel,
        (on_chip((BLOCKS, 3 * HALF, LANES), BF16), on_chip((4, 3 * HALF, LANES), F32)),
        (near(keep), near(swap_cores(give))),
    )
    parts = lax.all_to_all(sums.reshape(4, 4, 3 * HALF, LANES), "zl", split_axis=0, concat_axis=0, tiled=True)
    sums, own = call(
        near_kernel,
        (on_chip((4, 3 * HALF, LANES), BF16), on_chip((3 * HALF, LANES), F32)),
        (near(parts), near(own)),
    )
    parts = lax.all_to_all(sums, "zh", split_axis=0, concat_axis=0, tiled=True)
    piece = call(middle_kernel, on_chip((PIECE, LANES), BF16), (slot_gate, near(parts), near(own)))
    mine = lax.all_gather(piece, ("zh", "zl"), axis=0, tiled=False)
    other = swap_cores(mine)
    grad_gate, grad_up, grad_down, outgoing = call(
        back_kernel,
        (
            shape(gate_weight.shape, BF16),
            shape(up_weight.shape, BF16),
            shape(down_weight.shape, BF16),
            on_chip((OWNERS, ROOM, LANES), F32),
        ),
        (slot_tokens, near(inputs), near(scaled), near(mine), near(other), gate_weight, up_weight),
    )
    incoming = lax.all_to_all(outgoing, ("x", "y"), split_axis=0, concat_axis=0, tiled=True)
    grad_tokens, gate_line = call(
        last_kernel,
        (shape((TOK, LANES), BF16), shape((1, LANES), F32)),
        (slot_tokens, near(incoming)),
    )
    return (grad_tokens, grad_gate[None], grad_up[None], grad_down[None], gate_line[:, :40])


def solution(mesh):
    torus = Mesh(mesh.devices.reshape(4, 4, 2, 4, 4), ("zh", "zl", "core", "x", "y"))
    dp, expert = ("zh", "zl", "core"), ("x", "y")
    in_specs = (
        P(expert, dp),
        P(expert, dp),
        P(),
        P(),
        P(expert, dp, None),
        P(expert, dp, None),
        P(expert, None, dp),
    )
    out_specs = (
        P(expert, dp),
        P(expert, dp, None),
        P(expert, dp, None),
        P(expert, None, dp),
        P(expert, None),
    )
    return jax.shard_map(
        per_device, mesh=torus, in_specs=in_specs, out_specs=out_specs, check_vma=False
    )
```

```python
import jax
import jax.numpy as jnp
from jax import lax
from jax.experimental import pallas as pl
from jax.experimental.pallas import tpu as pltpu
from jax.sharding import Mesh
from jax.sharding import PartitionSpec as P

BF16 = jnp.bfloat16
F32 = jnp.float32
I32 = jnp.int32

TOK = 320
CAP = 160
HALF = 80
OWNERS = 16
FLIGHT = 4
MOST = 20
ROOM = 24
LANES = 128
BLOCKS = 16
PIECE = 3 * HALF + 8

Z = ("pair", "odd")
VMEM = pl.BlockSpec(memory_space=pltpu.VMEM)


def iota(shape, dim):
    return lax.broadcasted_iota(I32, shape, dim)


def dot(left, right, left_dim=1, right_dim=0, precision=None):
    return lax.dot_general(
        left,
        right,
        (((left_dim,), (right_dim,)), ((), ())),
        preferred_element_type=F32,
        precision=precision,
    )


def owned_tokens(row, first, rows, room):
    start = jnp.sum((row < first).astype(I32), axis=1, keepdims=True)
    count = jnp.sum(((row >= first) & (row < first + TOK)).astype(I32), axis=1, keepdims=True)
    rank = lax.rem(iota((rows, CAP), 0), room)
    chosen = (iota((rows, CAP), 1) == start + rank) & (rank < count)
    token = jnp.sum(jnp.where(chosen, row - first + 1, 0), axis=1, keepdims=True)
    return token - 1


def column(row, core):
    slot = lax.rem(iota((CAP, CAP), 0) + HALF * core, CAP)
    return jnp.sum(jnp.where(iota((CAP, CAP), 1) == slot, row, 0), axis=1, keepdims=True)


def places(row, core):
    token = column(row, core)
    owner = jnp.sum(
        ((iota((CAP, LANES), 1) < OWNERS - 1) & (token >= TOK * (iota((CAP, LANES), 1) + 1))).astype(I32),
        axis=1,
        keepdims=True,
    )
    start = jnp.sum((row < TOK * owner).astype(I32), axis=1, keepdims=True)
    slot = lax.rem(iota((CAP, 1), 0) + HALF * core, CAP)
    return owner, slot - start


def dispatch_kernel(
    slots_hbm,
    gates_hbm,
    tokens_hbm,
    grads_hbm,
    gate_hbm,
    up_hbm,
    down_hbm,
    send_ref,
    slots_ref,
    gates_ref,
    gate_ref,
    up_ref,
    down_ref,
    tokens_ref,
    grads_ref,
    sems,
):
    pairs = (
        (slots_hbm, slots_ref),
        (tokens_hbm, tokens_ref),
        (grads_hbm, grads_ref),
        (gates_hbm, gates_ref),
        (gate_hbm, gate_ref),
        (up_hbm, up_ref),
        (down_hbm, down_ref),
    )
    copies = [pltpu.make_async_copy(source, target, sems.at[i]) for i, (source, target) in enumerate(pairs)]
    for copy in copies:
        copy.start()
    for copy in copies[:3]:
        copy.wait()
    first = TOK * (4 * lax.axis_index("x") + lax.axis_index("y"))
    rows = 2 * MOST
    for expert in range(FLIGHT):
        local = owned_tokens(slots_ref[expert : expert + 1, :], first, rows, MOST)
        hit = local == iota((rows, TOK), 1)
        upper = iota((rows, TOK), 0) < MOST
        pick_tokens = jnp.where(hit & upper, 1.0, 0.0).astype(BF16)
        pick_grads = jnp.where(hit & ~upper, 1.0, 0.0).astype(BF16)
        rows_out = (dot(pick_tokens, tokens_ref[...]) + dot(pick_grads, grads_ref[...])).astype(BF16)
        for part in range(4):
            send_ref[4 * expert + part] = rows_out
    for copy in copies[3:]:
        copy.wait()


def front_kernel(
    slots_ref, gates_ref, recv_ref, gate_ref, up_ref, down_ref, keep_ref, send_ref, inputs_ref, scaled_ref
):
    expert = lax.axis_index("x")
    core = lax.axis_index("core")
    row = slots_ref[pl.ds(expert, 1), :]
    owner, rank = places(row, core)
    place = owner * (2 * MOST) + rank
    width = OWNERS * 2 * MOST
    recv = recv_ref[...].reshape(width, LANES)
    where = iota((CAP, width), 1)
    inputs = dot(jnp.where(where == place, 1.0, 0.0).astype(BF16), recv).astype(BF16)
    grads = dot(jnp.where(where == place + MOST, 1.0, 0.0).astype(BF16), recv)
    gates = column(gates_ref[pl.ds(expert, 1), :], core)
    scaled = (gates * grads).astype(BF16)
    inputs_ref[...] = inputs
    scaled_ref[...] = scaled
    for pair in range(BLOCKS // 2):
        cols = slice(256 * pair, 256 * pair + 256)
        sums = (
            dot(inputs, gate_ref[:, cols]),
            dot(inputs, up_ref[:, cols]),
            dot(scaled, down_ref[cols, :], 1, 1),
        )
        for which, total in enumerate(sums):
            for side in range(2):
                lanes = slice(LANES * side, LANES * side + LANES)
                rows = slice(HALF * which, HALF * which + HALF)
                keep_ref[2 * pair + side, rows, :] = total[:HALF, lanes]
                send_ref[2 * pair + side, rows, :] = total[HALF:, lanes]


def chip():
    return 2 * lax.axis_index("pair") + lax.axis_index("odd")


def pair_kernel(keep_ref, recv_ref, right_ref, left_ref, even_ref):
    def both(distance):
        block = lax.rem(chip() + distance + BLOCKS, BLOCKS)
        return keep_ref[block] + recv_ref[block]

    for step in range(4):
        right_ref[step] = both(1 + 2 * step).astype(BF16)
        left_ref[step] = both(-1 - 2 * step).astype(BF16)
    for step in range(8):
        even_ref[step] = both(2 * step)


def near_kernel(even_ref, from_left_ref, from_right_ref, sums_ref, own_ref):
    here = lax.axis_index("pair")
    for step in range(8):
        total = even_ref[step]
        if step < 4:
            total = total + from_left_ref[step].astype(F32)
        if step == 0 or step > 4:
            total = total + from_right_ref[(8 - step) % 8].astype(F32)
        if step == 0:
            own_ref[...] = total
        sums_ref[lax.rem(here + step, 8)] = total.astype(BF16)


def middle_kernel(gates_ref, parts_ref, own_ref, out_ref):
    core = lax.axis_index("core")
    gates = column(gates_ref[pl.ds(lax.axis_index("x"), 1), :], core)[:HALF]

    def total(which):
        rows = slice(HALF * which, HALF * which + HALF)
        result = own_ref[rows, :]
        for step in range(1, 8):
            result = result + parts_ref[lax.rem(lax.axis_index("pair") + step, 8), rows, :].astype(F32)
        return result

    pre_gate, pre_up, upstream = total(0), total(1), total(2)
    sigmoid = jax.nn.sigmoid(pre_gate)
    hidden = (pre_gate * sigmoid * pre_up).astype(BF16)
    out_ref[:HALF, :] = hidden
    out_ref[HALF : 2 * HALF, :] = (upstream * pre_up * sigmoid * (1.0 + pre_gate * (1.0 - sigmoid))).astype(BF16)
    out_ref[2 * HALF : 3 * HALF, :] = (upstream * pre_gate * sigmoid).astype(BF16)
    part = jnp.sum(hidden.astype(F32) * upstream, axis=1, keepdims=True) / gates
    eye = iota((HALF, LANES), 0) == iota((HALF, LANES), 1)
    part = jnp.sum(jnp.where(eye, part, 0.0), axis=0, keepdims=True)
    high = part.astype(BF16).astype(F32)
    line = iota((8, LANES), 0)
    tail = jnp.where(line == 0, high, jnp.where(line == 1, part - high, 0.0))
    out_ref[3 * HALF :, :] = tail.astype(BF16)


def back_kernel(
    slots_ref,
    inputs_ref,
    scaled_ref,
    mine_ref,
    other_ref,
    gate_ref,
    up_ref,
    grad_gate_ref,
    grad_up_ref,
    grad_down_ref,
    send_ref,
):
    core = lax.axis_index("core")
    inputs = inputs_ref[...]
    scaled = scaled_ref[...]

    def joined(which, pair):
        rows = slice(HALF * which, HALF * which + HALF)
        sides = [
            jnp.concatenate([mine_ref[place, rows, :], other_ref[place, rows, :]], axis=0)
            for place in (2 * pair, 2 * pair + 1)
        ]
        return jnp.concatenate(sides, axis=1)

    back = jnp.zeros((CAP, LANES), F32)
    for pair in range(BLOCKS // 2):
        cols = slice(256 * pair, 256 * pair + 256)
        hidden, gate_side, up_side = joined(0, pair), joined(1, pair), joined(2, pair)
        grad_gate_ref[:, cols] = dot(inputs, gate_side, 0, 0).astype(BF16)
        grad_up_ref[:, cols] = dot(inputs, up_side, 0, 0).astype(BF16)
        grad_down_ref[cols, :] = dot(hidden, scaled, 0, 0).astype(BF16)
        back = back + dot(gate_side, gate_ref[:, cols], 1, 1) + dot(up_side, up_ref[:, cols], 1, 1)

    row = slots_ref[pl.ds(lax.axis_index("x"), 1), :]
    owner, rank = places(row, core)
    spread = jnp.where(iota((CAP, OWNERS * ROOM), 1) == owner * ROOM + rank, 1.0, 0.0)
    buckets = dot(spread, back, 0, 0, lax.Precision.HIGHEST).reshape(OWNERS, ROOM, LANES)

    def gate_row(ref):
        lines = jnp.zeros((8, LANES), F32)
        for block in range(BLOCKS):
            lines = lines + ref[block, 3 * HALF :, :].astype(F32)
        return jnp.broadcast_to(jnp.sum(lines, axis=0, keepdims=True), (8, LANES))

    gates_mine, gates_other = gate_row(mine_ref), gate_row(other_ref)
    line = iota((8, LANES), 0)
    for quarter in range(4):
        slot = iota((LANES, LANES), 1) + 40 * quarter
        place = lax.rem(slot + HALF * core, CAP)
        source = iota((LANES, LANES), 0)
        valid = iota((LANES, LANES), 1) < 40
        take_mine = jnp.where(valid & (place < HALF) & (source == place), 1.0, 0.0)
        take_other = jnp.where(valid & (place >= HALF) & (source == place - HALF), 1.0, 0.0)
        gates = dot(gates_mine, take_mine, precision=lax.Precision.HIGHEST) + dot(
            gates_other, take_other, precision=lax.Precision.HIGHEST
        )
        for expert in range(FLIGHT):
            bucket = buckets[4 * expert + quarter]
            send_ref[4 * expert + quarter, :16, :] = bucket[:16]
            send_ref[4 * expert + quarter, 16:, :] = jnp.where(line == 4, gates, bucket[16:])


def last_kernel(slots_ref, incoming_ref, tokens_ref, gates_ref):
    expert_here = lax.axis_index("x")
    first = TOK * (4 * expert_here + lax.axis_index("y"))
    total = jnp.zeros((TOK, LANES), F32)
    for expert in range(FLIGHT):
        local = owned_tokens(slots_ref[expert : expert + 1, :], first, ROOM, ROOM)
        pick = jnp.where(local == iota((ROOM, TOK), 1), 1.0, 0.0)
        rows = incoming_ref[4 * expert]
        for part in range(1, 4):
            rows = rows + incoming_ref[4 * expert + part]
        total = total + dot(pick, rows, 0, 0, lax.Precision.HIGHEST)
    tokens_ref[...] = total.astype(BF16)
    gates = incoming_ref[4 * expert_here, 16:, :]
    for part in range(1, 4):
        gates = gates + incoming_ref[4 * expert_here + part, 16:, :]
    gates_ref[...] = gates[4:5, :]


def call(kernel, out_shape, inputs):
    return pl.pallas_call(
        kernel,
        out_shape=out_shape,
        in_specs=[VMEM] * len(inputs),
        out_specs=jax.tree.map(lambda _: VMEM, out_shape),
        compiler_params=pltpu.CompilerParams(vmem_limit_bytes=24 << 20),
    )(*inputs)


def shape(dims, kind):
    return jax.ShapeDtypeStruct(dims, kind)


def on_chip(dims, kind):
    return pltpu.VMEM(dims, kind)


def near(value):
    return pltpu.with_memory_space_constraint(value, pltpu.VMEM)


def swap_cores(value):
    return lax.ppermute(value, "core", [(0, 1), (1, 0)])


def far(value):
    return pltpu.with_memory_space_constraint(value, pltpu.HBM)


def shift(value, step):
    return lax.ppermute(value, Z, [(z, (z + step) % BLOCKS) for z in range(BLOCKS)])


def per_device(tokens, out_grad, slot_tokens, slot_gate, w_gate, w_up, w_down):
    send, slots, gates, gate_weight, up_weight, down_weight = pl.pallas_call(
        dispatch_kernel,
        out_shape=(
            on_chip((OWNERS, 2 * MOST, LANES), BF16),
            on_chip(slot_tokens.shape, I32),
            on_chip(slot_gate.shape, F32),
            on_chip(w_gate.shape[1:], BF16),
            on_chip(w_up.shape[1:], BF16),
            on_chip(w_down.shape[1:], BF16),
        ),
        in_specs=[pl.BlockSpec(memory_space=pltpu.HBM)] * 7,
        out_specs=(VMEM,) * 6,
        scratch_shapes=[
            pltpu.VMEM(tokens.shape, BF16),
            pltpu.VMEM(tokens.shape, BF16),
            pltpu.SemaphoreType.DMA((7,)),
        ],
        compiler_params=pltpu.CompilerParams(vmem_limit_bytes=24 << 20),
    )(*(far(value) for value in (slot_tokens, slot_gate, tokens, out_grad, w_gate[0], w_up[0], w_down[0])))
    slots, gates, gate_weight, up_weight, down_weight = (
        near(value) for value in (slots, gates, gate_weight, up_weight, down_weight)
    )
    recv = lax.all_to_all(send, ("x", "y"), split_axis=0, concat_axis=0, tiled=True)
    halves = on_chip((BLOCKS, 3 * HALF, LANES), F32)
    rows = on_chip((CAP, LANES), BF16)
    keep, give, inputs, scaled = call(
        front_kernel,
        (halves, halves, rows, rows),
        (slots, gates, near(recv), gate_weight, up_weight, down_weight),
    )
    quarter = on_chip((4, 3 * HALF, LANES), BF16)
    right, left, even = call(
        pair_kernel,
        (quarter, quarter, on_chip((8, 3 * HALF, LANES), F32)),
        (near(keep), near(swap_cores(give))),
    )
    from_left, from_right = shift(right, 1), shift(left, -1)
    sums, own = call(
        near_kernel,
        (on_chip((8, 3 * HALF, LANES), BF16), on_chip((3 * HALF, LANES), F32)),
        (near(even), near(from_left), near(from_right)),
    )
    parts = lax.all_to_all(sums, "pair", split_axis=0, concat_axis=0, tiled=True)
    piece = call(middle_kernel, on_chip((PIECE, LANES), BF16), (gates, near(parts), near(own)))
    mine = lax.all_gather(piece, Z, axis=0, tiled=False)
    other = swap_cores(mine)
    grad_gate, grad_up, grad_down, outgoing = call(
        back_kernel,
        (
            shape(gate_weight.shape, BF16),
            shape(up_weight.shape, BF16),
            shape(down_weight.shape, BF16),
            on_chip((OWNERS, ROOM, LANES), F32),
        ),
        (slots, near(inputs), near(scaled), near(mine), near(other), gate_weight, up_weight),
    )
    incoming = lax.all_to_all(outgoing, ("x", "y"), split_axis=0, concat_axis=0, tiled=True)
    grad_tokens, gate_line = call(
        last_kernel,
        (shape((TOK, LANES), BF16), shape((1, LANES), F32)),
        (slots, near(incoming)),
    )
    return (grad_tokens, grad_gate[None], grad_up[None], grad_down[None], gate_line[:, :40])


def solution(mesh):
    torus = Mesh(mesh.devices.reshape(8, 2, 2, 4, 4), ("pair", "odd", "core", "x", "y"))
    dp, expert = (*Z, "core"), ("x", "y")
    in_specs = (
        P(expert, dp),
        P(expert, dp),
        P(),
        P(),
        P(expert, dp, None),
        P(expert, dp, None),
        P(expert, None, dp),
    )
    out_specs = (
        P(expert, dp),
        P(expert, dp, None),
        P(expert, dp, None),
        P(expert, None, dp),
        P(expert, None),
    )
    return jax.shard_map(
        per_device, mesh=torus, in_specs=in_specs, out_specs=out_specs, check_vma=False
    )
```

```python
import jax
import jax.numpy as jnp
from jax import lax
from jax.experimental import pallas as pl
from jax.experimental.pallas import tpu as pltpu
from jax.sharding import Mesh
from jax.sharding import PartitionSpec as P

BF16 = jnp.bfloat16
F32 = jnp.float32
I32 = jnp.int32

TOK = 320
CAP = 160
HALF = 80
OWNERS = 16
FLIGHT = 4
MOST = 20
ROOM = 24
LANES = 128
BLOCKS = 16
PIECE = 3 * HALF + 8

Z = ("pair", "odd")
VMEM = pl.BlockSpec(memory_space=pltpu.VMEM)


def iota(shape, dim):
    return lax.broadcasted_iota(I32, shape, dim)


def dot(left, right, left_dim=1, right_dim=0, precision=None):
    return lax.dot_general(
        left,
        right,
        (((left_dim,), (right_dim,)), ((), ())),
        preferred_element_type=F32,
        precision=precision,
    )


def owned_tokens(row, first, rows, room):
    start = jnp.sum((row < first).astype(I32), axis=1, keepdims=True)
    count = jnp.sum(((row >= first) & (row < first + TOK)).astype(I32), axis=1, keepdims=True)
    rank = lax.rem(iota((rows, CAP), 0), room)
    chosen = (iota((rows, CAP), 1) == start + rank) & (rank < count)
    token = jnp.sum(jnp.where(chosen, row - first + 1, 0), axis=1, keepdims=True)
    return token - 1


def column(row, core):
    slot = lax.rem(iota((CAP, CAP), 0) + HALF * core, CAP)
    return jnp.sum(jnp.where(iota((CAP, CAP), 1) == slot, row, 0), axis=1, keepdims=True)


def places(row, core):
    token = column(row, core)
    owner = jnp.sum(
        ((iota((CAP, LANES), 1) < OWNERS - 1) & (token >= TOK * (iota((CAP, LANES), 1) + 1))).astype(I32),
        axis=1,
        keepdims=True,
    )
    start = jnp.sum((row < TOK * owner).astype(I32), axis=1, keepdims=True)
    slot = lax.rem(iota((CAP, 1), 0) + HALF * core, CAP)
    return owner, slot - start


def dispatch_kernel(
    slots_hbm,
    gates_hbm,
    tokens_hbm,
    grads_hbm,
    gate_hbm,
    up_hbm,
    down_hbm,
    send_ref,
    slots_ref,
    gates_ref,
    gate_ref,
    up_ref,
    down_ref,
    tokens_ref,
    grads_ref,
    sems,
):
    pairs = (
        (slots_hbm, slots_ref),
        (tokens_hbm, tokens_ref),
        (grads_hbm, grads_ref),
        (gates_hbm, gates_ref),
        (gate_hbm, gate_ref),
        (up_hbm, up_ref),
        (down_hbm, down_ref),
    )
    copies = [pltpu.make_async_copy(source, target, sems.at[i]) for i, (source, target) in enumerate(pairs)]
    for copy in copies:
        copy.start()
    for copy in copies[:3]:
        copy.wait()
    first = TOK * (4 * lax.axis_index("x") + lax.axis_index("y"))
    rows = 2 * MOST
    for expert in range(FLIGHT):
        local = owned_tokens(slots_ref[expert : expert + 1, :], first, rows, MOST)
        hit = local == iota((rows, TOK), 1)
        upper = iota((rows, TOK), 0) < MOST
        pick_tokens = jnp.where(hit & upper, 1.0, 0.0).astype(BF16)
        pick_grads = jnp.where(hit & ~upper, 1.0, 0.0).astype(BF16)
        rows_out = (dot(pick_tokens, tokens_ref[...]) + dot(pick_grads, grads_ref[...])).astype(BF16)
        for part in range(4):
            send_ref[4 * expert + part] = rows_out
    for copy in copies[3:]:
        copy.wait()


def front_kernel(
    slots_ref, gates_ref, recv_ref, gate_ref, up_ref, down_ref, keep_ref, send_ref, inputs_ref, scaled_ref
):
    expert = lax.axis_index("x")
    core = lax.axis_index("core")
    row = slots_ref[pl.ds(expert, 1), :]
    owner, rank = places(row, core)
    place = owner * (2 * MOST) + rank
    width = OWNERS * 2 * MOST
    recv = recv_ref[...].reshape(width, LANES)
    where = iota((CAP, width), 1)
    inputs = dot(jnp.where(where == place, 1.0, 0.0).astype(BF16), recv).astype(BF16)
    grads = dot(jnp.where(where == place + MOST, 1.0, 0.0).astype(BF16), recv)
    gates = column(gates_ref[pl.ds(expert, 1), :], core)
    scaled = (gates * grads).astype(BF16)
    inputs_ref[...] = inputs
    scaled_ref[...] = scaled
    for pair in range(BLOCKS // 2):
        cols = slice(256 * pair, 256 * pair + 256)
        sums = (
            dot(inputs, gate_ref[:, cols]),
            dot(inputs, up_ref[:, cols]),
            dot(scaled, down_ref[cols, :], 1, 1),
        )
        for which, total in enumerate(sums):
            for side in range(2):
                lanes = slice(LANES * side, LANES * side + LANES)
                rows = slice(HALF * which, HALF * which + HALF)
                keep_ref[2 * pair + side, rows, :] = total[:HALF, lanes]
                send_ref[2 * pair + side, rows, :] = total[HALF:, lanes].astype(BF16)


def pair_kernel(keep_ref, recv_ref, give_ref, even_ref):
    odd = lax.axis_index("odd")

    def both(block):
        return keep_ref[block] + recv_ref[block].astype(F32)

    for pair in range(8):
        give_ref[pair] = both(2 * pair + 1 - odd).astype(BF16)
        even_ref[pair] = both(2 * pair + odd)


def near_kernel(even_ref, recv_ref, sums_ref, own_ref):
    here = lax.axis_index("pair")
    for pair in range(8):
        sums_ref[pair] = (even_ref[pair] + recv_ref[pair].astype(F32)).astype(BF16)
    own_ref[...] = even_ref[here] + recv_ref[here].astype(F32)


def middle_kernel(gates_ref, parts_ref, own_ref, out_ref):
    core = lax.axis_index("core")
    gates = column(gates_ref[pl.ds(lax.axis_index("x"), 1), :], core)[:HALF]

    def total(which):
        rows = slice(HALF * which, HALF * which + HALF)
        result = own_ref[rows, :]
        for step in range(1, 8):
            result = result + parts_ref[lax.rem(lax.axis_index("pair") + step, 8), rows, :].astype(F32)
        return result

    pre_gate, pre_up, upstream = total(0), total(1), total(2)
    sigmoid = jax.nn.sigmoid(pre_gate)
    hidden = (pre_gate * sigmoid * pre_up).astype(BF16)
    out_ref[:HALF, :] = hidden
    out_ref[HALF : 2 * HALF, :] = (upstream * pre_up * sigmoid * (1.0 + pre_gate * (1.0 - sigmoid))).astype(BF16)
    out_ref[2 * HALF : 3 * HALF, :] = (upstream * pre_gate * sigmoid).astype(BF16)
    part = jnp.sum(hidden.astype(F32) * upstream, axis=1, keepdims=True) / gates
    eye = iota((HALF, LANES), 0) == iota((HALF, LANES), 1)
    part = jnp.sum(jnp.where(eye, part, 0.0), axis=0, keepdims=True)
    high = part.astype(BF16).astype(F32)
    line = iota((8, LANES), 0)
    tail = jnp.where(line == 0, high, jnp.where(line == 1, part - high, 0.0))
    out_ref[3 * HALF :, :] = tail.astype(BF16)


def joined(mine_ref, other_ref, which, pair):
    rows = slice(HALF * which, HALF * which + HALF)
    sides = [
        jnp.concatenate([mine_ref[place, rows, :], other_ref[place, rows, :]], axis=0)
        for place in (2 * pair, 2 * pair + 1)
    ]
    return jnp.concatenate(sides, axis=1)


def grads_kernel(inputs_ref, scaled_ref, mine_ref, other_ref, grad_gate_ref, grad_up_ref, grad_down_ref):
    inputs = inputs_ref[...]
    scaled = scaled_ref[...]
    for pair in range(BLOCKS // 2):
        cols = slice(256 * pair, 256 * pair + 256)
        hidden, gate_side, up_side = (joined(mine_ref, other_ref, which, pair) for which in range(3))
        grad_gate_ref[:, cols] = dot(inputs, gate_side, 0, 0).astype(BF16)
        grad_up_ref[:, cols] = dot(inputs, up_side, 0, 0).astype(BF16)
        grad_down_ref[cols, :] = dot(hidden, scaled, 0, 0).astype(BF16)


def back_kernel(slots_ref, mine_ref, other_ref, gate_ref, up_ref, send_ref):
    core = lax.axis_index("core")
    back = jnp.zeros((CAP, LANES), F32)
    for pair in range(BLOCKS // 2):
        cols = slice(256 * pair, 256 * pair + 256)
        gate_side, up_side = (joined(mine_ref, other_ref, which, pair) for which in (1, 2))
        back = back + dot(gate_side, gate_ref[:, cols], 1, 1) + dot(up_side, up_ref[:, cols], 1, 1)

    row = slots_ref[pl.ds(lax.axis_index("x"), 1), :]
    owner, rank = places(row, core)
    spread = jnp.where(iota((CAP, OWNERS * ROOM), 1) == owner * ROOM + rank, 1.0, 0.0)
    buckets = dot(spread, back, 0, 0, lax.Precision.HIGHEST).reshape(OWNERS, ROOM, LANES)

    def gate_row(ref):
        lines = jnp.zeros((8, LANES), F32)
        for block in range(BLOCKS):
            lines = lines + ref[block, 3 * HALF :, :].astype(F32)
        return jnp.broadcast_to(jnp.sum(lines, axis=0, keepdims=True), (8, LANES))

    gates_mine, gates_other = gate_row(mine_ref), gate_row(other_ref)
    line = iota((8, LANES), 0)
    for quarter in range(4):
        slot = iota((LANES, LANES), 1) + 40 * quarter
        place = lax.rem(slot + HALF * core, CAP)
        source = iota((LANES, LANES), 0)
        valid = iota((LANES, LANES), 1) < 40
        take_mine = jnp.where(valid & (place < HALF) & (source == place), 1.0, 0.0)
        take_other = jnp.where(valid & (place >= HALF) & (source == place - HALF), 1.0, 0.0)
        gates = dot(gates_mine, take_mine, precision=lax.Precision.HIGHEST) + dot(
            gates_other, take_other, precision=lax.Precision.HIGHEST
        )
        for expert in range(FLIGHT):
            bucket = buckets[4 * expert + quarter]
            send_ref[4 * expert + quarter, :16, :] = bucket[:16]
            send_ref[4 * expert + quarter, 16:, :] = jnp.where(line == 4, gates, bucket[16:])


def last_kernel(slots_ref, incoming_ref, tokens_ref, gates_ref):
    expert_here = lax.axis_index("x")
    first = TOK * (4 * expert_here + lax.axis_index("y"))
    total = jnp.zeros((TOK, LANES), F32)
    for expert in range(FLIGHT):
        local = owned_tokens(slots_ref[expert : expert + 1, :], first, ROOM, ROOM)
        pick = jnp.where(local == iota((ROOM, TOK), 1), 1.0, 0.0)
        rows = incoming_ref[4 * expert]
        for part in range(1, 4):
            rows = rows + incoming_ref[4 * expert + part]
        total = total + dot(pick, rows, 0, 0, lax.Precision.HIGHEST)
    tokens_ref[...] = total.astype(BF16)
    gates = incoming_ref[4 * expert_here, 16:, :]
    for part in range(1, 4):
        gates = gates + incoming_ref[4 * expert_here + part, 16:, :]
    gates_ref[...] = gates[4:5, :]


def call(kernel, out_shape, inputs):
    return pl.pallas_call(
        kernel,
        out_shape=out_shape,
        in_specs=[VMEM] * len(inputs),
        out_specs=jax.tree.map(lambda _: VMEM, out_shape),
        compiler_params=pltpu.CompilerParams(vmem_limit_bytes=24 << 20),
    )(*inputs)


def shape(dims, kind):
    return jax.ShapeDtypeStruct(dims, kind)


def on_chip(dims, kind):
    return pltpu.VMEM(dims, kind)


def near(value):
    return pltpu.with_memory_space_constraint(value, pltpu.VMEM)


def swap_cores(value):
    return lax.ppermute(value, "core", [(0, 1), (1, 0)])


def far(value):
    return pltpu.with_memory_space_constraint(value, pltpu.HBM)


def swap_chips(value):
    return lax.ppermute(value, Z, [(z, z ^ 1) for z in range(BLOCKS)])


def per_device(tokens, out_grad, slot_tokens, slot_gate, w_gate, w_up, w_down):
    send, slots, gates, gate_weight, up_weight, down_weight = pl.pallas_call(
        dispatch_kernel,
        out_shape=(
            on_chip((OWNERS, 2 * MOST, LANES), BF16),
            on_chip(slot_tokens.shape, I32),
            on_chip(slot_gate.shape, F32),
            on_chip(w_gate.shape[1:], BF16),
            on_chip(w_up.shape[1:], BF16),
            on_chip(w_down.shape[1:], BF16),
        ),
        in_specs=[pl.BlockSpec(memory_space=pltpu.HBM)] * 7,
        out_specs=(VMEM,) * 6,
        scratch_shapes=[
            pltpu.VMEM(tokens.shape, BF16),
            pltpu.VMEM(tokens.shape, BF16),
            pltpu.SemaphoreType.DMA((7,)),
        ],
        compiler_params=pltpu.CompilerParams(vmem_limit_bytes=24 << 20),
    )(*(far(value) for value in (slot_tokens, slot_gate, tokens, out_grad, w_gate[0], w_up[0], w_down[0])))
    slots, gates, gate_weight, up_weight, down_weight = (
        near(value) for value in (slots, gates, gate_weight, up_weight, down_weight)
    )
    recv = lax.all_to_all(send, ("x", "y"), split_axis=0, concat_axis=0, tiled=True)
    halves = (BLOCKS, 3 * HALF, LANES)
    rows = on_chip((CAP, LANES), BF16)
    keep, give, inputs, scaled = call(
        front_kernel,
        (on_chip(halves, F32), on_chip(halves, BF16), rows, rows),
        (slots, gates, near(recv), gate_weight, up_weight, down_weight),
    )
    part = (8, 3 * HALF, LANES)
    give, even = call(
        pair_kernel, (on_chip(part, BF16), on_chip(part, F32)), (near(keep), near(swap_cores(give)))
    )
    sums, own = call(
        near_kernel,
        (on_chip(part, BF16), on_chip((3 * HALF, LANES), F32)),
        (near(even), near(swap_chips(give))),
    )
    parts = lax.all_to_all(sums, "pair", split_axis=0, concat_axis=0, tiled=True)
    piece = call(middle_kernel, on_chip((PIECE, LANES), BF16), (gates, near(parts), near(own)))
    mine = lax.all_gather(piece, Z, axis=0, tiled=False)
    other = swap_cores(mine)
    mine, other = near(mine), near(other)
    outgoing = call(
        back_kernel,
        on_chip((OWNERS, ROOM, LANES), F32),
        (slots, mine, other, gate_weight, up_weight),
    )
    grad_gate, grad_up, grad_down = call(
        grads_kernel,
        (shape(gate_weight.shape, BF16), shape(up_weight.shape, BF16), shape(down_weight.shape, BF16)),
        (near(inputs), near(scaled), mine, other),
    )
    incoming = lax.all_to_all(outgoing, ("x", "y"), split_axis=0, concat_axis=0, tiled=True)
    grad_tokens, gate_line = call(
        last_kernel,
        (shape((TOK, LANES), BF16), shape((1, LANES), F32)),
        (slots, near(incoming)),
    )
    return (grad_tokens, grad_gate[None], grad_up[None], grad_down[None], gate_line[:, :40])


def solution(mesh):
    torus = Mesh(mesh.devices.reshape(8, 2, 2, 4, 4), ("pair", "odd", "core", "x", "y"))
    dp, expert = (*Z, "core"), ("x", "y")
    in_specs = (
        P(expert, dp),
        P(expert, dp),
        P(),
        P(),
        P(expert, dp, None),
        P(expert, dp, None),
        P(expert, None, dp),
    )
    out_specs = (
        P(expert, dp),
        P(expert, dp, None),
        P(expert, dp, None),
        P(expert, None, dp),
        P(expert, None),
    )
    return jax.shard_map(
        per_device, mesh=torus, in_specs=in_specs, out_specs=out_specs, check_vma=False
    )
```

```python
import jax
import jax.numpy as jnp
from jax import lax
from jax.experimental import pallas as pl
from jax.experimental.pallas import tpu as pltpu
from jax.sharding import Mesh
from jax.sharding import PartitionSpec as P

BF16 = jnp.bfloat16
F32 = jnp.float32
I32 = jnp.int32

TOK = 320
CAP = 160
HALF = 80
OWNERS = 16
FLIGHT = 4
MOST = 20
ROOM = 24
LANES = 128
CHIPS = 16
BLOCKS = 8
PIECE = 3 * HALF + 8

Z = ("pair", "odd")
VMEM = pl.BlockSpec(memory_space=pltpu.VMEM)


def iota(shape, dim):
    return lax.broadcasted_iota(I32, shape, dim)


def dot(left, right, left_dim=1, right_dim=0, precision=None):
    return lax.dot_general(
        left,
        right,
        (((left_dim,), (right_dim,)), ((), ())),
        preferred_element_type=F32,
        precision=precision,
    )


def owned_tokens(row, first, rows, room):
    start = jnp.sum((row < first).astype(I32), axis=1, keepdims=True)
    count = jnp.sum(((row >= first) & (row < first + TOK)).astype(I32), axis=1, keepdims=True)
    rank = lax.rem(iota((rows, CAP), 0), room)
    chosen = (iota((rows, CAP), 1) == start + rank) & (rank < count)
    token = jnp.sum(jnp.where(chosen, row - first + 1, 0), axis=1, keepdims=True)
    return token - 1


def column(row, odd):
    slot = lax.rem(iota((CAP, CAP), 0) + HALF * odd, CAP)
    return jnp.sum(jnp.where(iota((CAP, CAP), 1) == slot, row, 0), axis=1, keepdims=True)


def places(row, odd):
    token = column(row, odd)
    owner = jnp.sum(
        ((iota((CAP, LANES), 1) < OWNERS - 1) & (token >= TOK * (iota((CAP, LANES), 1) + 1))).astype(I32),
        axis=1,
        keepdims=True,
    )
    start = jnp.sum((row < TOK * owner).astype(I32), axis=1, keepdims=True)
    slot = lax.rem(iota((CAP, 1), 0) + HALF * odd, CAP)
    return owner, slot - start


def block_of(core, block):
    return pl.ds(pl.multiple_of((BLOCKS * core + block) * LANES, LANES), LANES)


def dispatch_kernel(
    slots_hbm,
    gates_hbm,
    tokens_hbm,
    grads_hbm,
    gate_hbm,
    up_hbm,
    down_hbm,
    send_ref,
    slots_ref,
    gates_ref,
    have_ref,
    give_ref,
    tokens_ref,
    grads_ref,
    sems,
):
    core = lax.axis_index("core")
    pairs = [
        (slots_hbm, slots_ref),
        (tokens_hbm, tokens_ref),
        (grads_hbm, grads_ref),
        (gates_hbm, gates_ref),
    ]
    for side, target in ((1 - core, give_ref), (core, have_ref)):
        for block in range(BLOCKS):
            pairs.append((gate_hbm.at[:, block_of(side, block)], target.at[0, block]))
            pairs.append((up_hbm.at[:, block_of(side, block)], target.at[1, block]))
            pairs.append((down_hbm.at[block_of(side, block), :], target.at[2, block]))
    copies = [pltpu.make_async_copy(source, target, sems.at[i]) for i, (source, target) in enumerate(pairs)]
    for copy in copies:
        copy.start()
    for copy in copies[:3]:
        copy.wait()
    first = TOK * (4 * lax.axis_index("x") + lax.axis_index("y"))
    rows = 2 * MOST
    for expert in range(FLIGHT):
        local = owned_tokens(slots_ref[expert : expert + 1, :], first, rows, MOST)
        hit = local == iota((rows, TOK), 1)
        upper = iota((rows, TOK), 0) < MOST
        pick_tokens = jnp.where(hit & upper, 1.0, 0.0).astype(BF16)
        pick_grads = jnp.where(hit & ~upper, 1.0, 0.0).astype(BF16)
        rows_out = (dot(pick_tokens, tokens_ref[...]) + dot(pick_grads, grads_ref[...])).astype(BF16)
        for side in range(2):
            for part in range(4):
                send_ref[OWNERS * side + 4 * expert + part] = rows_out
    for copy in copies[3:]:
        copy.wait()


def tile(have_ref, other_ref, which, blocks):
    axis = 1 if which == 2 else 0
    return jnp.concatenate(
        [
            jnp.concatenate([ref[which, block] for block in blocks], axis=1 - axis)
            for ref in (have_ref, other_ref)
        ],
        axis=axis,
    )


def front_kernel(
    slots_ref, gates_ref, recv_ref, have_ref, other_ref, even_ref, right_ref, left_ref, inputs_ref, scaled_ref
):
    expert = lax.axis_index("x")
    core = lax.axis_index("core")
    odd = lax.axis_index("odd")
    row = slots_ref[pl.ds(expert, 1), :]
    owner, rank = places(row, odd)
    place = owner * (2 * MOST) + rank
    width = OWNERS * 2 * MOST
    where = iota((CAP, width), 1)
    pick_inputs = jnp.where(where == place, 1.0, 0.0).astype(BF16)
    pick_grads = jnp.where(where == place + MOST, 1.0, 0.0).astype(BF16)
    gates = column(gates_ref[pl.ds(expert, 1), :], odd)
    for index, side in enumerate((core, 1 - core)):
        recv = recv_ref[pl.ds(OWNERS * side, OWNERS)].reshape(width, LANES)
        lanes = slice(LANES * index, LANES * index + LANES)
        inputs_ref[:, lanes] = dot(pick_inputs, recv).astype(BF16)
        scaled_ref[:, lanes] = (gates * dot(pick_grads, recv)).astype(BF16)
    inputs = inputs_ref[...]
    scaled = scaled_ref[...]
    for pair in range(BLOCKS // 2):
        steps = (2 * pair, 2 * pair + 1)
        blocks = [lax.rem(lax.axis_index("pair") + odd + step, BLOCKS) for step in steps]
        sums = (
            dot(inputs, tile(have_ref, other_ref, 0, blocks)),
            dot(inputs, tile(have_ref, other_ref, 1, blocks)),
            dot(scaled, tile(have_ref, other_ref, 2, blocks), 1, 1),
        )
        give_ref = right_ref if pair < 2 else left_ref
        for which, total in enumerate(sums):
            rows = slice(HALF * which, HALF * which + HALF)
            for side in range(2):
                lanes = slice(LANES * side, LANES * side + LANES)
                even_ref[blocks[side], rows, :] = total[:HALF, lanes]
                give_ref[steps[side] % 4, rows, :] = total[HALF:, lanes].astype(BF16)


def near_kernel(even_ref, from_left_ref, from_right_ref, sums_ref, own_ref):
    here = lax.axis_index("pair")
    for step in range(BLOCKS):
        block = lax.rem(here + step, BLOCKS)
        total = even_ref[block]
        if step < 4:
            total = total + from_left_ref[step].astype(F32)
        if step == 0 or step > 4:
            total = total + from_right_ref[3 - (BLOCKS - step) % BLOCKS].astype(F32)
        if step == 0:
            own_ref[...] = total
        sums_ref[block] = total.astype(BF16)


def middle_kernel(gates_ref, parts_ref, own_ref, out_ref):
    gates = column(gates_ref[pl.ds(lax.axis_index("x"), 1), :], lax.axis_index("odd"))[:HALF]

    def total(which):
        rows = slice(HALF * which, HALF * which + HALF)
        result = own_ref[rows, :]
        for step in range(1, BLOCKS):
            result = result + parts_ref[lax.rem(lax.axis_index("pair") + step, BLOCKS), rows, :].astype(F32)
        return result

    pre_gate, pre_up, upstream = total(0), total(1), total(2)
    sigmoid = jax.nn.sigmoid(pre_gate)
    hidden = (pre_gate * sigmoid * pre_up).astype(BF16)
    out_ref[:HALF, :] = hidden
    out_ref[HALF : 2 * HALF, :] = (upstream * pre_up * sigmoid * (1.0 + pre_gate * (1.0 - sigmoid))).astype(BF16)
    out_ref[2 * HALF : 3 * HALF, :] = (upstream * pre_gate * sigmoid).astype(BF16)
    part = jnp.sum(hidden.astype(F32) * upstream, axis=1, keepdims=True) / gates
    eye = iota((HALF, LANES), 0) == iota((HALF, LANES), 1)
    part = jnp.sum(jnp.where(eye, part, 0.0), axis=0, keepdims=True)
    high = part.astype(BF16).astype(F32)
    line = iota((8, LANES), 0)
    tail = jnp.where(line == 0, high, jnp.where(line == 1, part - high, 0.0))
    out_ref[3 * HALF :, :] = tail.astype(BF16)


def back_kernel(
    slots_ref, inputs_ref, scaled_ref, parts_ref, have_ref, other_ref, own_ref, give_ref, send_ref
):
    core = lax.axis_index("core")
    odd = lax.axis_index("odd")
    inputs = inputs_ref[...]
    scaled = scaled_ref[...]

    def joined(which, blocks):
        rows = slice(HALF * which, HALF * which + HALF)
        return jnp.concatenate(
            [
                jnp.concatenate([parts_ref[2 * block + half, rows, :] for half in (odd, 1 - odd)], axis=0)
                for block in blocks
            ],
            axis=1,
        )

    first, second = slice(0, LANES), slice(LANES, 2 * LANES)
    back = jnp.zeros((CAP, 2 * LANES), F32)
    for pair in range(BLOCKS // 2):
        blocks = (2 * pair, 2 * pair + 1)
        hidden, gate_side, up_side = joined(0, blocks), joined(1, blocks), joined(2, blocks)
        for which, side in ((0, gate_side), (1, up_side)):
            grad = dot(inputs, side, 0, 0).astype(BF16)
            for block, cols in zip(blocks, (first, second)):
                own_ref[which, block] = grad[first, cols]
                give_ref[which, block] = grad[second, cols]
            back = back + dot(side, tile(have_ref, other_ref, which, blocks), 1, 1)
        grad = dot(hidden, scaled, 0, 0).astype(BF16)
        for block, rows in zip(blocks, (first, second)):
            own_ref[2, block] = grad[rows, first]
            give_ref[2, block] = grad[rows, second]

    row = slots_ref[pl.ds(lax.axis_index("x"), 1), :]
    owner, rank = places(row, odd)
    spread = jnp.where(iota((CAP, OWNERS * ROOM), 1) == owner * ROOM + rank, 1.0, 0.0)
    buckets = dot(spread, back, 0, 0, lax.Precision.HIGHEST)

    def gate_row(half):
        lines = jnp.zeros((8, LANES), F32)
        for block in range(BLOCKS):
            lines = lines + parts_ref[2 * block + half, 3 * HALF :, :].astype(F32)
        return jnp.broadcast_to(jnp.sum(lines, axis=0, keepdims=True), (8, LANES))

    halves = [gate_row(half) for half in range(2)]
    line = iota((8, LANES), 0)
    for quarter in range(4):
        slot = iota((LANES, LANES), 1) + 40 * quarter
        valid = iota((LANES, LANES), 1) < 40
        gates = jnp.zeros((8, LANES), F32)
        for half in range(2):
            take = jnp.where(valid & (iota((LANES, LANES), 0) + HALF * half == slot), 1.0, 0.0)
            take = jnp.where(iota((LANES, LANES), 0) < HALF, take, 0.0)
            gates = gates + dot(halves[half], take, precision=lax.Precision.HIGHEST)
        for expert in range(FLIGHT):
            place = 4 * expert + quarter
            for side, lanes in ((core, first), (1 - core, second)):
                bucket = buckets[ROOM * place : ROOM * place + ROOM, lanes]
                send_ref[OWNERS * side + place, :16, :] = bucket[:16]
                send_ref[OWNERS * side + place, 16:, :] = jnp.where(line == 4, gates, bucket[16:])


def last_kernel(
    slots_ref,
    incoming_ref,
    own_ref,
    other_ref,
    tokens_ref,
    gates_ref,
    grad_gate_hbm,
    grad_up_hbm,
    grad_down_hbm,
    sems,
):
    core = lax.axis_index("core")
    pairs = []
    for side, source in ((core, own_ref), (1 - core, other_ref)):
        for block in range(BLOCKS):
            pairs.append((source.at[0, block], grad_gate_hbm.at[:, block_of(side, block)]))
            pairs.append((source.at[1, block], grad_up_hbm.at[:, block_of(side, block)]))
            pairs.append((source.at[2, block], grad_down_hbm.at[block_of(side, block), :]))
    copies = [pltpu.make_async_copy(source, target, sems.at[i]) for i, (source, target) in enumerate(pairs)]
    for copy in copies:
        copy.start()

    def arrived(expert, rows):
        parts = [incoming_ref[OWNERS * side + 4 * expert + part, rows, :] for side in range(2) for part in range(4)]
        total = parts[0]
        for part in parts[1:]:
            total = total + part
        return total

    expert_here = lax.axis_index("x")
    first = TOK * (4 * expert_here + lax.axis_index("y"))
    total = jnp.zeros((TOK, LANES), F32)
    for expert in range(FLIGHT):
        local = owned_tokens(slots_ref[expert : expert + 1, :], first, ROOM, ROOM)
        pick = jnp.where(local == iota((ROOM, TOK), 1), 1.0, 0.0)
        total = total + dot(pick, arrived(expert, slice(0, ROOM)), 0, 0, lax.Precision.HIGHEST)
    tokens_ref[...] = total.astype(BF16)
    gates_ref[...] = arrived(expert_here, slice(16, ROOM))[4:5, :]
    for copy in copies:
        copy.wait()


def call(kernel, out_shape, inputs):
    return pl.pallas_call(
        kernel,
        out_shape=out_shape,
        in_specs=[VMEM] * len(inputs),
        out_specs=jax.tree.map(lambda _: VMEM, out_shape),
        compiler_params=pltpu.CompilerParams(vmem_limit_bytes=24 << 20),
    )(*inputs)


def shape(dims, kind):
    return jax.ShapeDtypeStruct(dims, kind)


def on_chip(dims, kind):
    return pltpu.VMEM(dims, kind)


def near(value):
    return pltpu.with_memory_space_constraint(value, pltpu.VMEM)


def swap_cores(value):
    return lax.ppermute(value, "core", [(0, 1), (1, 0)])


def far(value):
    return pltpu.with_memory_space_constraint(value, pltpu.HBM)


def shift(value, step):
    return lax.ppermute(value, Z, [(z, (z + step) % CHIPS) for z in range(CHIPS)])


def per_device(tokens, out_grad, slot_tokens, slot_gate, w_gate, w_up, w_down):
    weights = (3, BLOCKS, LANES, LANES)
    send, slots, gates, have, give = pl.pallas_call(
        dispatch_kernel,
        out_shape=(
            on_chip((2 * OWNERS, 2 * MOST, LANES), BF16),
            on_chip(slot_tokens.shape, I32),
            on_chip(slot_gate.shape, F32),
            on_chip(weights, BF16),
            on_chip(weights, BF16),
        ),
        in_specs=[pl.BlockSpec(memory_space=pltpu.HBM)] * 7,
        out_specs=(VMEM,) * 5,
        scratch_shapes=[
            pltpu.VMEM(tokens.shape, BF16),
            pltpu.VMEM(tokens.shape, BF16),
            pltpu.SemaphoreType.DMA((4 + 6 * BLOCKS,)),
        ],
        compiler_params=pltpu.CompilerParams(vmem_limit_bytes=24 << 20),
    )(*(far(value) for value in (slot_tokens, slot_gate, tokens, out_grad, w_gate[0], w_up[0], w_down[0])))
    slots, gates, have, other = near(slots), near(gates), near(have), near(swap_cores(give))
    everyone = ("core", "x", "y")
    recv = lax.all_to_all(send, everyone, split_axis=0, concat_axis=0, tiled=True)
    part = (BLOCKS, 3 * HALF, LANES)
    quarter = on_chip((4, 3 * HALF, LANES), BF16)
    rows = on_chip((CAP, 2 * LANES), BF16)
    even, right, left, inputs, scaled = call(
        front_kernel,
        (on_chip(part, F32), quarter, quarter, rows, rows),
        (slots, gates, near(recv), have, other),
    )
    from_left, from_right = shift(right, 1), shift(left, -1)
    sums, own = call(
        near_kernel,
        (on_chip(part, BF16), on_chip((3 * HALF, LANES), F32)),
        (near(even), near(from_left), near(from_right)),
    )
    parts = lax.all_to_all(sums, "pair", split_axis=0, concat_axis=0, tiled=True)
    piece = call(middle_kernel, on_chip((PIECE, LANES), BF16), (gates, near(parts), near(own)))
    pieces = lax.all_gather(piece, Z, axis=0, tiled=False)
    mine, give, outgoing = call(
        back_kernel,
        (on_chip(weights, BF16), on_chip(weights, BF16), on_chip((2 * OWNERS, ROOM, LANES), F32)),
        (slots, near(inputs), near(scaled), near(pieces), have, other),
    )
    incoming = lax.all_to_all(outgoing, everyone, split_axis=0, concat_axis=0, tiled=True)
    grad_tokens, gate_line, grad_gate, grad_up, grad_down = pl.pallas_call(
        last_kernel,
        out_shape=(
            shape((TOK, LANES), BF16),
            shape((1, LANES), F32),
            shape(w_gate.shape[1:], BF16),
            shape(w_up.shape[1:], BF16),
            shape(w_down.shape[1:], BF16),
        ),
        in_specs=[VMEM] * 4,
        out_specs=(VMEM, VMEM) + (pl.BlockSpec(memory_space=pltpu.HBM),) * 3,
        scratch_shapes=[pltpu.SemaphoreType.DMA((6 * BLOCKS,))],
        compiler_params=pltpu.CompilerParams(vmem_limit_bytes=24 << 20),
    )(slots, near(incoming), near(mine), near(swap_cores(give)))
    return (grad_tokens, grad_gate[None], grad_up[None], grad_down[None], gate_line[:, :40])


def solution(mesh):
    torus = Mesh(mesh.devices.reshape(8, 2, 2, 4, 4), ("pair", "odd", "core", "x", "y"))
    dp, expert = (*Z, "core"), ("x", "y")
    in_specs = (
        P(expert, dp),
        P(expert, dp),
        P(),
        P(),
        P(expert, dp, None),
        P(expert, dp, None),
        P(expert, None, dp),
    )
    out_specs = (
        P(expert, dp),
        P(expert, dp, None),
        P(expert, dp, None),
        P(expert, None, dp),
        P(expert, None),
    )
    return jax.shard_map(
        per_device, mesh=torus, in_specs=in_specs, out_specs=out_specs, check_vma=False
    )
```
